256 devices in a mesh: wide: 16 (over x, y_lo, core), loop: 16 (over y_hi, z).
Axes of the slice: x: 4, y: 4 (y_hi: 2, y_lo: 2; y = y_hi * 2 + y_lo), z: 8, core: 2. Of those that a mesh axis runs over, the one named last changes fastest.
Arguments:
- query_grads: bfloat16 [65536, 16384], P('loop', 'wide'), may hold values from -6 to 6
- train_grads: bfloat16 [640, 16384], P('loop', 'wide'), may hold values from -0.046875 to 0.046875
- precond: bfloat16 [2048, 16384], P(None, 'wide'), may hold values from -3 to 3
Outputs:
- scores: float32 [65536, 640], P(('loop', 'wide'))
The draws below stay inside these ranges and needn't reach their ends.
All inputs are finite; a program needn't handle non-finite values.
Results may differ from the reference program's by a relative error of at most 0.0029.
Values may be sent and summed in bfloat16 or wider, within the bound.
No kernel may reach another device: no remote copies, remote signals or barrier semaphores. Data moves between devices by JAX's collectives and lax.ppermute only.
A program may use at most 128 MiB of HBM per device.

```python
import math
import jax
import jax.numpy as jnp
from jax import lax

BS = 2048
NB = 8
FEAT = 16384
NQ = 65536
NT = 640


def draw_precond(key, part):
    key_noise, key_diag = jax.random.split(jax.random.fold_in(key, 7))
    noise_part = jnp.clip(jax.random.normal(key_noise, (BS, FEAT), jnp.float32), -4.0, 4.0)
    diag_scale = jnp.exp(jax.random.uniform(key_diag, (FEAT,), jnp.float32, -0.69, 0.69))
    row_index = lax.broadcasted_iota(jnp.int32, (BS, FEAT), 0)
    col_index = lax.broadcasted_iota(jnp.int32, (BS, FEAT), 1)
    on_diag = (col_index % BS == row_index).astype(jnp.float32)
    return (on_diag * diag_scale[None, :] + noise_part * (0.6 / math.sqrt(BS))).astype(jnp.bfloat16)


def spiked(entries, rng, source, target, shards_of, factor):
    owner, partner = [(jnp.arange(entries.shape[axis_at]) // (entries.shape[axis_at] // shards_of)).reshape([-1 if axis == axis_at else 1 for axis in range(entries.ndim)]) for axis_at in (source, target)]
    chosen = jax.random.permutation(rng, shards_of)[partner]
    strong = (owner == chosen) | (owner == (partner + shards_of // 2) % shards_of)
    return jnp.where(strong, factor * entries, entries)


def shard_levels(own_key, shape, pieces, least, largest):
    def one(dim, blocks):
        heights = jax.random.uniform(jax.random.fold_in(jax.random.fold_in(own_key, 6), dim), (blocks,), jnp.float32, least / len(pieces), largest / len(pieces))
        return jnp.repeat(jnp.exp(heights), shape[dim] // blocks).reshape((-1,) + (1,) * (len(shape) - dim - 1))

    loudness = one(*pieces[0])
    for cut in pieces[1:]:
        loudness = loudness * one(*cut)
    return loudness


def scatter_about(key, extent, deviation, limit, cuts=(), dtype=jnp.bfloat16):
    level = shard_levels(key, extent, cuts, -0.22, 0.18) if cuts else 1.0
    result = jax.random.normal(key, extent, jnp.float32) * deviation * level
    return jnp.minimum(jnp.maximum(result, -limit), limit).astype(dtype)


def gaussian_with(stream_key, extent, deviation, limit, pieces, heavy, dtype=jnp.bfloat16):
    drawn = deviation * jax.random.normal(stream_key, extent, jnp.float32)
    if pieces:
        drawn = drawn * shard_levels(stream_key, extent, pieces, -0.22, 0.18)
    return jnp.clip(spiked(drawn, jax.random.fold_in(stream_key, 3), *heavy), -limit, limit).astype(dtype)


def setup_inputs(seed: int = 0) -> dict:
    splits = jax.random.split(jax.random.key(seed), 4)
    query_grads = gaussian_with(splits[0], (NQ, FEAT), 1.0, 6.0, ((0, 16), (1, 16)), (1, 0, 16, 2.0))
    train_grads = scatter_about(splits[1], (NT, FEAT), FEAT ** -0.5, 0.046875, ((0, 16), (1, 16)))
    precond = draw_precond(jax.random.fold_in(splits[3], 71), 0)
    return dict(query_grads=query_grads, train_grads=train_grads, precond=precond)


def reference(query_grads, train_grads, precond):
    train_blocks = train_grads.astype(jnp.float32).reshape(NT, NB, BS)
    factor_blocks = precond.astype(jnp.float32).reshape(BS, NB, BS)
    conditioned = jnp.einsum("tbi,ibj->tbj", train_blocks, factor_blocks, precision=lax.Precision.HIGHEST)
    conditioned = conditioned.reshape(NT, FEAT).astype(jnp.bfloat16)
    return lax.dot_general(query_grads, conditioned, (((1,), (1,)), ((), ())), preferred_element_type=jnp.float32)
```

```python
import jax
import jax.numpy as jnp
from jax import lax
from jax.experimental import pallas as pl
from jax.experimental.pallas import tpu as pltpu
from jax.sharding import Mesh, PartitionSpec as P

DOT_NT = (((1,), (1,)), ((), ()))


def permute(block, axis, target):
    count = lax.axis_size(axis)
    return lax.ppermute(block, axis, [(i, target(i) % count) for i in range(count)])


def partial_scores_kernel(core_ref, own_rows_ref, mate_rows_ref, own_q_ref, mate_q_ref, out_ref):
    total = lax.dot_general(
        own_rows_ref[...], own_q_ref[...], DOT_NT, preferred_element_type=jnp.float32
    )
    total += lax.dot_general(
        mate_rows_ref[...], mate_q_ref[...], DOT_NT, preferred_element_type=jnp.float32
    )
    out_ref[...] = total.astype(jnp.bfloat16)[None]


def partial_scores(core, own_rows, mate_rows, own_q, mate_q, chips):
    rows, depth = own_rows.shape
    owned = own_q.shape[0] // (2 * chips)
    whole = pl.BlockSpec((rows, depth), lambda d, core_ref: (0, 0))
    queries = pl.BlockSpec((owned, depth), lambda d, core_ref: (2 * d + core_ref[0], 0))
    return pl.pallas_call(
        partial_scores_kernel,
        grid_spec=pltpu.PrefetchScalarGridSpec(
            num_scalar_prefetch=1,
            grid=(chips,),
            in_specs=[whole, whole, queries, queries],
            out_specs=pl.BlockSpec((1, rows, owned), lambda d, core_ref: (d, 0, 0)),
        ),
        out_shape=jax.ShapeDtypeStruct((chips, rows, owned), jnp.bfloat16),
        compiler_params=pltpu.CompilerParams(vmem_limit_bytes=32 * 2**20),
        cost_estimate=pl.CostEstimate(
            flops=4 * chips * owned * rows * depth,
            bytes_accessed=4 * chips * owned * depth + 4 * rows * depth + 2 * chips * owned * rows,
            transcendentals=0,
        ),
        name="partial_scores",
    )(core, own_rows, mate_rows, own_q, mate_q)


def total_scores_kernel(depth_z, block, z_ref, parts_ref, out_ref, placed_ref):
    chips = parts_ref.shape[0]
    half = depth_z * block
    for step in range(depth_z):
        z = lax.rem(z_ref[0] + step, depth_z)
        rows = pl.ds(step * 2 * block, 2 * block)
        total = parts_ref[0, rows, :].astype(jnp.float32)
        for chip in range(1, chips):
            total += parts_ref[chip, rows, :].astype(jnp.float32)
        for side in range(2):
            first = pl.multiple_of(side * half + z * block, 8)
            placed_ref[pl.ds(first, block), :] = total[side * block : (side + 1) * block]
    out_ref[...] = placed_ref[...].T


def total_scores(z, parts, block):
    chips, rows, owned = parts.shape
    return pl.pallas_call(
        lambda *refs: total_scores_kernel(rows // (2 * block), block, *refs),
        grid_spec=pltpu.PrefetchScalarGridSpec(
            num_scalar_prefetch=1,
            grid=(1,),
            in_specs=[pl.BlockSpec((chips, rows, owned), lambda i, z_ref: (0, 0, 0))],
            out_specs=pl.BlockSpec((owned, rows), lambda i, z_ref: (0, 0)),
            scratch_shapes=[pltpu.VMEM((rows, owned), jnp.float32)],
        ),
        out_shape=jax.ShapeDtypeStruct((owned, rows), jnp.float32),
        compiler_params=pltpu.CompilerParams(vmem_limit_bytes=32 * 2**20),
        name="total_scores",
    )(z, parts)


def shards(query_grads, train_grads, precond):
    core, y_hi, z = lax.axis_index("core"), lax.axis_index("y_hi"), lax.axis_index("z")

    def other_core(block):
        return permute(block, "core", lambda i: 1 - i)

    train_mate = other_core(train_grads)
    query_mate = other_core(query_grads)
    train_block = jnp.where(
        core == 1,
        jnp.concatenate([train_mate, train_grads], axis=1),
        jnp.concatenate([train_grads, train_mate], axis=1),
    )
    own = jnp.dot(train_block, precond, preferred_element_type=jnp.float32).astype(jnp.bfloat16)

    far = permute(own, "y_hi", lambda i: 1 - i)
    here = jnp.where(y_hi == 1, jnp.concatenate([far, own]), jnp.concatenate([own, far]))
    ahead1 = permute(here, "z", lambda i: i - 1)
    behind1 = permute(here, "z", lambda i: i + 1)
    across = permute(here, "z", lambda i: i + 4)
    ahead = permute(jnp.concatenate([ahead1, across]), "z", lambda i: i - 1)
    behind = permute(jnp.concatenate([across, behind1]), "z", lambda i: i + 1)
    rows = here.shape[0]
    conditioned = jnp.concatenate(
        [here, ahead1, ahead[:rows], behind[:rows], across, ahead[rows:], behind[rows:], behind1]
    )
    conditioned_mate = other_core(conditioned)

    chips = lax.axis_size("x") * lax.axis_size("y_lo")
    parts = partial_scores(
        core.reshape(1), conditioned, conditioned_mate, query_grads, query_mate, chips
    )
    parts = lax.all_to_all(parts, ("x", "y_lo"), split_axis=0, concat_axis=0, tiled=True)
    return total_scores(z.reshape(1), parts, own.shape[0])


def solution(mesh):
    split = Mesh(mesh.devices.reshape(4, 2, 2, 2, 8), ("x", "y_lo", "core", "y_hi", "z"))
    wide, loop = ("x", "y_lo", "core"), ("y_hi", "z")
    return jax.shard_map(
        shards,
        mesh=split,
        in_specs=(P(loop, wide), P(loop, wide), P(None, wide)),
        out_specs=P(loop + wide, None),
        check_vma=False,
    )
```

```python
import jax
import jax.numpy as jnp
from jax import lax
from jax.experimental import pallas as pl
from jax.experimental.pallas import tpu as pltpu
from jax.sharding import Mesh, PartitionSpec as P

DOT_NT = (((1,), (1,)), ((), ()))


def permute(block, axis, target):
    count = lax.axis_size(axis)
    return lax.ppermute(block, axis, [(i, target(i) % count) for i in range(count)])


def partial_scores_kernel(core_ref, own_rows_ref, mate_rows_ref, own_q_ref, mate_q_ref, out_ref):
    total = lax.dot_general(
        own_rows_ref[...], own_q_ref[...], DOT_NT, preferred_element_type=jnp.float32
    )
    total += lax.dot_general(
        mate_rows_ref[...], mate_q_ref[...], DOT_NT, preferred_element_type=jnp.float32
    )
    out_ref[...] = total.astype(jnp.bfloat16)[None]


def partial_scores(core, own_rows, mate_rows, own_q, mate_q, chips):
    rows, depth = own_rows.shape
    owned = own_q.shape[0] // (2 * chips)
    whole = pl.BlockSpec((rows, depth), lambda d, core_ref: (0, 0))
    queries = pl.BlockSpec((owned, depth), lambda d, core_ref: (2 * d + core_ref[0], 0))
    return pl.pallas_call(
        partial_scores_kernel,
        grid_spec=pltpu.PrefetchScalarGridSpec(
            num_scalar_prefetch=1,
            grid=(chips,),
            in_specs=[whole, whole, queries, queries],
            out_specs=pl.BlockSpec((1, rows, owned), lambda d, core_ref: (d, 0, 0)),
        ),
        out_shape=jax.ShapeDtypeStruct((chips, rows, owned), jnp.bfloat16),
        compiler_params=pltpu.CompilerParams(vmem_limit_bytes=56 * 2**20),
        cost_estimate=pl.CostEstimate(
            flops=4 * chips * owned * rows * depth,
            bytes_accessed=4 * chips * owned * depth + 4 * rows * depth + 2 * chips * owned * rows,
            transcendentals=0,
        ),
        name="partial_scores",
    )(core, own_rows, mate_rows, own_q, mate_q)


def total_scores_kernel(steps, block, z_ref, *refs):
    parts_refs, out_ref, placed_ref = refs[:-2], refs[-2], refs[-1]
    depth_z = sum(len(part) for part in steps)
    half = depth_z * block
    for parts_ref, part in zip(parts_refs, steps):
        for place, step in enumerate(part):
            z = lax.rem(z_ref[0] + step, depth_z)
            rows = pl.ds(place * 2 * block, 2 * block)
            total = parts_ref[0, rows, :].astype(jnp.float32)
            for chip in range(1, parts_ref.shape[0]):
                total += parts_ref[chip, rows, :].astype(jnp.float32)
            for side in range(2):
                first = pl.multiple_of(side * half + z * block, 8)
                placed_ref[pl.ds(first, block), :] = total[side * block : (side + 1) * block]
    out_ref[...] = placed_ref[...].T


def total_scores(z, parts, steps, block):
    owned = parts[0].shape[2]
    rows = sum(part.shape[1] for part in parts)
    return pl.pallas_call(
        lambda *refs: total_scores_kernel(steps, block, *refs),
        grid_spec=pltpu.PrefetchScalarGridSpec(
            num_scalar_prefetch=1,
            grid=(1,),
            in_specs=[pl.BlockSpec(part.shape, lambda i, z_ref: (0, 0, 0)) for part in parts],
            out_specs=pl.BlockSpec((owned, rows), lambda i, z_ref: (0, 0)),
            scratch_shapes=[pltpu.VMEM((rows, owned), jnp.float32)],
        ),
        out_shape=jax.ShapeDtypeStruct((owned, rows), jnp.float32),
        compiler_params=pltpu.CompilerParams(vmem_limit_bytes=32 * 2**20),
        cost_estimate=pl.CostEstimate(
            flops=8 * rows * owned, bytes_accessed=20 * rows * owned, transcendentals=0
        ),
        name="total_scores",
    )(z, *parts)


def shards(query_grads, train_grads, precond):
    core, y_hi, z = lax.axis_index("core"), lax.axis_index("y_hi"), lax.axis_index("z")

    def other_core(block):
        return permute(block, "core", lambda i: 1 - i)

    def scores_of(rows):
        parts = partial_scores(
            core.reshape(1), rows, other_core(rows), query_grads, query_mate, chips
        )
        return lax.all_to_all(parts, ("x", "y_lo"), split_axis=0, concat_axis=0, tiled=True)

    chips = lax.axis_size("x") * lax.axis_size("y_lo")
    train_mate = other_core(train_grads)
    query_sent, train_mate = lax.optimization_barrier((query_grads, train_mate))
    query_mate = other_core(query_sent)
    train_block = jnp.where(
        core == 1,
        jnp.concatenate([train_mate, train_grads], axis=1),
        jnp.concatenate([train_grads, train_mate], axis=1),
    )
    own = jnp.dot(train_block, precond, preferred_element_type=jnp.float32).astype(jnp.bfloat16)

    far = permute(own, "y_hi", lambda i: 1 - i)
    here = jnp.where(y_hi == 1, jnp.concatenate([far, own]), jnp.concatenate([own, far]))
    ahead1 = permute(here, "z", lambda i: i - 1)
    behind1 = permute(here, "z", lambda i: i + 1)
    across = permute(here, "z", lambda i: i + 4)
    ahead = permute(jnp.concatenate([ahead1, across]), "z", lambda i: i - 1)
    behind = permute(jnp.concatenate([across, behind1]), "z", lambda i: i + 1)
    near_parts = scores_of(jnp.concatenate([here, ahead1, across, behind1]))
    rest_parts = scores_of(jnp.concatenate([ahead, behind]))
    steps = ((0, 1, 4, 7), (2, 5, 3, 6))
    return total_scores(z.reshape(1), (near_parts, rest_parts), steps, own.shape[0])


def solution(mesh):
    split = Mesh(mesh.devices.reshape(4, 2, 2, 2, 8), ("x", "y_lo", "core", "y_hi", "z"))
    wide, loop = ("x", "y_lo", "core"), ("y_hi", "z")
    return jax.shard_map(
        shards,
        mesh=split,
        in_specs=(P(loop, wide), P(loop, wide), P(None, wide)),
        out_specs=P(loop + wide, None),
        check_vma=False,
    )
```

```python
import jax
import jax.numpy as jnp
from jax import lax
from jax.experimental import pallas as pl
from jax.experimental.pallas import tpu as pltpu
from jax.sharding import Mesh, PartitionSpec as P

def permute(block, axis, target):
    count = lax.axis_size(axis)
    return lax.ppermute(block, axis, [(i, target(i) % count) for i in range(count)])


def scores_against(rows, queries):
    return lax.dot_general(
        rows, queries, (((1,), (1,)), ((), ())), preferred_element_type=jnp.float32
    )


def total_scores_kernel(steps, block, z_ref, *refs):
    chunk_refs, out_ref, placed_ref = refs[:-2], refs[-2], refs[-1]
    depth_z = sum(len(chunk) for chunk in steps)
    half = depth_z * block
    for index, chunk in enumerate(steps):
        count = len(chunk_refs) // len(steps)
        parts = chunk_refs[index * count : (index + 1) * count]
        for place, step in enumerate(chunk):
            z = lax.rem(z_ref[0] + step, depth_z)
            rows = pl.ds(place * 2 * block, 2 * block)
            total = parts[0][rows, :]
            for part in parts[1:]:
                total += part[rows, :].astype(jnp.float32)
            for side in range(2):
                first = pl.multiple_of(side * half + z * block, 8)
                placed_ref[pl.ds(first, block), :] = total[side * block : (side + 1) * block]
    out_ref[...] = placed_ref[...].T


def total_scores(z, chunks, steps, block):
    owned = chunks[0][0].shape[1]
    rows = sum(chunk[0].shape[0] for chunk in chunks)
    parts = [part for chunk in chunks for part in chunk]
    return pl.pallas_call(
        lambda *refs: total_scores_kernel(steps, block, *refs),
        grid_spec=pltpu.PrefetchScalarGridSpec(
            num_scalar_prefetch=1,
            grid=(1,),
            in_specs=[pl.BlockSpec(part.shape, lambda i, z_ref: (0, 0)) for part in parts],
            out_specs=pl.BlockSpec((owned, rows), lambda i, z_ref: (0, 0)),
            scratch_shapes=[pltpu.VMEM((rows, owned), jnp.float32)],
        ),
        out_shape=jax.ShapeDtypeStruct((owned, rows), jnp.float32),
        compiler_params=pltpu.CompilerParams(vmem_limit_bytes=16 * 2**20),
        cost_estimate=pl.CostEstimate(
            flops=8 * rows * owned, bytes_accessed=20 * rows * owned, transcendentals=0
        ),
        name="total_scores",
    )(z, *parts)


def shards(query_grads, train_grads, precond):
    core, y_hi, z = lax.axis_index("core"), lax.axis_index("y_hi"), lax.axis_index("z")

    def other_core(block):
        return permute(block, "core", lambda i: 1 - i)

    def scored_here(queries):
        by_owner = queries.reshape(count_x, count_y, 2, -1, queries.shape[1])
        blocks = []
        for step_x, step_y in owners:
            start = ((x + step_x) % count_x, (y_lo + step_y) % count_y, core, 0, 0)
            size = (1, 1, 1) + by_owner.shape[3:]
            blocks.append(lax.dynamic_slice(by_owner, start, size).reshape(size[3:]))
        return blocks

    def to_owner(part, step_x, step_y):
        route = []
        for i in range(count_x * count_y):
            to_x, to_y = (i // count_y + step_x) % count_x, (i % count_y + step_y) % count_y
            route.append((i, to_x * count_y + to_y))
        return lax.ppermute(part, ("x", "y_lo"), route)

    def totals_of(rows):
        mate_rows = other_core(rows)
        parts = []
        for (step_x, step_y), own_block, mate_block in zip(owners, own_q, mate_q):
            part = scores_against(rows, own_block) + scores_against(mate_rows, mate_block)
            if step_x or step_y:
                part = to_owner(part.astype(jnp.bfloat16), step_x, step_y)
            parts.append(part)
        return parts[-1:] + parts[:-1]

    count_x, count_y = lax.axis_size("x"), lax.axis_size("y_lo")
    x, y_lo = lax.axis_index("x"), lax.axis_index("y_lo")
    owners = [(2, 1), (1, 1), (3, 1), (2, 0), (0, 1), (1, 0), (3, 0), (0, 0)]
    train_mate = other_core(train_grads)
    query_sent, train_mate = lax.optimization_barrier((query_grads, train_mate))
    query_mate = other_core(query_sent)
    train_block = jnp.where(
        core == 1,
        jnp.concatenate([train_mate, train_grads], axis=1),
        jnp.concatenate([train_grads, train_mate], axis=1),
    )
    own = jnp.dot(train_block, precond, preferred_element_type=jnp.float32).astype(jnp.bfloat16)

    far = permute(own, "y_hi", lambda i: 1 - i)
    own_q = scored_here(lax.optimization_barrier((query_grads, own))[0])
    *own_q, far = lax.optimization_barrier((*own_q, far))
    here = jnp.where(y_hi == 1, jnp.concatenate([far, own]), jnp.concatenate([own, far]))
    ahead1 = permute(here, "z", lambda i: i - 1)
    behind1 = permute(here, "z", lambda i: i + 1)
    across = permute(here, "z", lambda i: i + 4)
    mate_q = scored_here(query_mate)
    *mate_q, ahead1 = lax.optimization_barrier((*mate_q, ahead1))
    ahead = permute(jnp.concatenate([ahead1, across]), "z", lambda i: i - 1)
    behind = permute(jnp.concatenate([across, behind1]), "z", lambda i: i + 1)
    near = totals_of(jnp.concatenate([here, ahead1, across, behind1]))
    near[1], ahead, behind = lax.optimization_barrier((near[1], ahead, behind))
    rest = totals_of(jnp.concatenate([ahead, behind]))
    steps = ((0, 1, 4, 7), (2, 5, 3, 6))
    return total_scores(z.reshape(1), (near, rest), steps, own.shape[0])


def solution(mesh):
    split = Mesh(mesh.devices.reshape(4, 2, 2, 2, 8), ("x", "y_lo", "core", "y_hi", "z"))
    wide, loop = ("x", "y_lo", "core"), ("y_hi", "z")
    return jax.shard_map(
        shards,
        mesh=split,
        in_specs=(P(loop, wide), P(loop, wide), P(None, wide)),
        out_specs=P(loop + wide, None),
        check_vma=False,
    )
```

```python
import jax
import jax.numpy as jnp
from jax import lax
from jax.experimental import pallas as pl
from jax.experimental.pallas import tpu as pltpu
from jax.sharding import Mesh, PartitionSpec as P
def permute(block, axis, target):
    count = lax.axis_size(axis)
    return lax.ppermute(block, axis, [(i, target(i) % count) for i in range(count)])


def scores_against(rows, queries):
    return jnp.einsum("tf,dqf->tdq", rows, queries, preferred_element_type=jnp.float32)


def total_scores_kernel(steps, block, z_ref, *refs):
    part_refs, out_ref, placed_ref = refs[:-2], refs[-2], refs[-1]
    half = len(steps) * block
    for place, step in enumerate(steps):
        total = None
        for first_pair, part_ref in part_refs:
            row = (place - first_pair) * 2 * block
            if 0 <= row < part_ref.shape[1]:
                for chip in range(part_ref.shape[0]):
                    part = part_ref[chip, pl.ds(row, 2 * block), :].astype(jnp.float32)
                    total = part if total is None else total + part
        z = lax.rem(z_ref[0] + step, len(steps))
        for side in range(2):
            first = pl.multiple_of(side * half + z * block, 8)
            placed_ref[pl.ds(first, block), :] = total[side * block : (side + 1) * block]
    out_ref[...] = placed_ref[...].T


def total_scores(z, parts, steps, block):
    owned = parts[0][1].shape[2]
    rows = 2 * block * len(steps)
    firsts = [first for first, _ in parts]
    blocks = [part for _, part in parts]

    def kernel(z_ref, *refs):
        count = len(firsts)
        total_scores_kernel(steps, block, z_ref, *zip(firsts, refs[:count]), *refs[count:])

    return pl.pallas_call(
        kernel,
        grid_spec=pltpu.PrefetchScalarGridSpec(
            num_scalar_prefetch=1,
            grid=(1,),
            in_specs=[pl.BlockSpec(part.shape, lambda i, z_ref: (0, 0, 0)) for part in blocks],
            out_specs=pl.BlockSpec((owned, rows), lambda i, z_ref: (0, 0)),
            scratch_shapes=[pltpu.VMEM((rows, owned), jnp.float32)],
        ),
        out_shape=jax.ShapeDtypeStruct((owned, rows), jnp.float32),
        compiler_params=pltpu.CompilerParams(vmem_limit_bytes=16 * 2**20),
        cost_estimate=pl.CostEstimate(
            flops=8 * rows * owned, bytes_accessed=20 * rows * owned, transcendentals=0
        ),
        name="total_scores",
    )(z, *blocks)


def shards(query_grads, train_grads, precond):
    core, y_hi, z = lax.axis_index("core"), lax.axis_index("y_hi"), lax.axis_index("z")

    def other_core(block):
        return permute(block, "core", lambda i: 1 - i)

    def scored_here(queries):
        by_owner = queries.reshape(count_x * count_y, 2, -1, queries.shape[1])
        return lax.dynamic_index_in_dim(by_owner, core, axis=1, keepdims=False)

    def to_owner(part, step_x, step_y):
        route = []
        for i in range(count_x * count_y):
            to_x, to_y = (i // count_y + step_x) % count_x, (i % count_y + step_y) % count_y
            route.append((i, to_x * count_y + to_y))
        return lax.ppermute(part, ("x", "y_lo"), route)

    def scores_of(rows):
        parts = scores_against(rows, own_q) + scores_against(other_core(rows), mate_q)
        return parts.astype(jnp.bfloat16).transpose(1, 0, 2)

    count_x, count_y = lax.axis_size("x"), lax.axis_size("y_lo")
    x, y_lo = lax.axis_index("x"), lax.axis_index("y_lo")
    owners = [(2, 1), (1, 1), (3, 1), (2, 0), (0, 1), (1, 0), (3, 0), (0, 0)]
    train_mate = other_core(train_grads)
    query_sent, train_mate = lax.optimization_barrier((query_grads, train_mate))
    query_mate = other_core(query_sent)
    train_block = jnp.where(
        core == 1,
        jnp.concatenate([train_mate, train_grads], axis=1),
        jnp.concatenate([train_grads, train_mate], axis=1),
    )
    own = jnp.dot(train_block, precond, preferred_element_type=jnp.float32).astype(jnp.bfloat16)

    far = permute(own, "y_hi", lambda i: 1 - i)
    own_q = scored_here(lax.optimization_barrier((query_grads, own))[0])
    own_q, far = lax.optimization_barrier((own_q, far))
    here = jnp.where(y_hi == 1, jnp.concatenate([far, own]), jnp.concatenate([own, far]))
    ahead1 = permute(here, "z", lambda i: i - 1)
    behind1 = permute(here, "z", lambda i: i + 1)
    across = permute(here, "z", lambda i: i + 4)
    mate_q = scored_here(query_mate)
    mate_q, ahead1 = lax.optimization_barrier((mate_q, ahead1))
    ahead = permute(jnp.concatenate([ahead1, across]), "z", lambda i: i - 1)
    behind = permute(jnp.concatenate([across, behind1]), "z", lambda i: i + 1)
    near = scores_of(jnp.concatenate([here, ahead1, across, behind1]))
    near, ahead, behind = lax.optimization_barrier((near, ahead, behind))
    near = lax.all_to_all(near, ("x", "y_lo"), split_axis=0, concat_axis=0, tiled=True)
    rest = scores_of(jnp.concatenate([ahead, behind]))
    parts = [(0, near)]
    for step_x, step_y in owners:
        owner = (x + step_x) % count_x * count_y + (y_lo + step_y) % count_y
        part = lax.dynamic_slice_in_dim(rest, owner, 1)
        if step_x or step_y:
            part = to_owner(part, step_x, step_y)
        parts.append((4, part))
    steps = (0, 1, 4, 7, 2, 5, 3, 6)
    return total_scores(z.reshape(1), parts, steps, own.shape[0])


def solution(mesh):
    split = Mesh(mesh.devices.reshape(4, 2, 2, 2, 8), ("x", "y_lo", "core", "y_hi", "z"))
    wide, loop = ("x", "y_lo", "core"), ("y_hi", "z")
    return jax.shard_map(
        shards,
        mesh=split,
        in_specs=(P(loop, wide), P(loop, wide), P(None, wide)),
        out_specs=P(loop + wide, None),
        check_vma=False,
    )
```
